32 devices in a mesh: row: 4 (over z_hi, core), col: 4 (over y, x), depth: 2 (over z_lo).
Axes of the slice: x: 2, y: 2, z: 4 (z_hi: 2, z_lo: 2; z = z_hi * 2 + z_lo), core: 2. Of those that a mesh axis runs over, the one named last changes fastest.
Arguments:
- matrix: bfloat16 [20480, 20480], P(('col', 'depth'), 'row'), may hold values from 0 to 250, as said below
- swaps: int32 [512], replicated, may hold values from 512 to 20479, as said below
- inverse_first: bfloat16 [256, 256], replicated, may hold values from 0 to 250, as said below
- inverse_second: bfloat16 [256, 256], replicated, may hold values from 0 to 250, as said below
Outputs:
- updated: bfloat16 [20480, 20480], P(('col', 'depth'), 'row')
The draws below stay inside these ranges and needn't reach their ends.
Inputs may be any that keep to these rules, and one draw needn't show every extreme that they name: `matrix`: whole numbers. Whole numbers; inverse_first times the block of permuted at rows and columns 0 to 255 is the identity modulo 251. Whole numbers; inverse_second times the block of first_update at rows and columns 256 to 511 is the identity modulo 251. `swaps`: distinct rows, none below 512.
All inputs are finite; a program needn't handle non-finite values.
Results may differ from the reference program's by a relative error of at most 0.001.
Values may be sent and summed in bfloat16 or wider, within the bound.
No kernel may reach another device: no remote copies, remote signals or barrier semaphores. Data moves between devices by JAX's collectives and lax.ppermute only.
A program may use at most 320 MiB of HBM per device.

```python
import jax
import jax.numpy as jnp
from jax import lax

M = 20480
PB = 256


def residues(key, shape):
    return jax.random.randint(key, shape, 0, 251).astype(jnp.int32)


def product_mod(left_part, right_part):
    return jnp.mod(jnp.dot(left_part, right_part), 251).astype(jnp.int32)


def negated(values):
    return jnp.mod(251 - values, 251).astype(jnp.int32)


def elementary(block_part, upper_side):
    half_width = PB // 2
    identity_half = jnp.eye(half_width, dtype=jnp.int32)
    zeros_half = jnp.zeros((half_width, half_width), jnp.int32)
    if upper_side:
        top_half = jnp.concatenate([identity_half, block_part], axis=1)
        low_half = jnp.concatenate([zeros_half, identity_half], axis=1)
    else:
        top_half = jnp.concatenate([identity_half, zeros_half], axis=1)
        low_half = jnp.concatenate([block_part, identity_half], axis=1)
    return jnp.concatenate([top_half, low_half], axis=0)


def invertible_pair(key, salt_value):
    half_width = PB // 2
    first_factor = residues(jax.random.fold_in(key, salt_value), (half_width, half_width))
    second_factor = residues(jax.random.fold_in(key, salt_value + 1), (half_width, half_width))
    third_factor = residues(jax.random.fold_in(key, salt_value + 2), (half_width, half_width))
    forward = product_mod(product_mod(elementary(first_factor, True), elementary(second_factor, False)), elementary(third_factor, True))
    backward = product_mod(product_mod(elementary(negated(third_factor), True), elementary(negated(second_factor), False)), elementary(negated(first_factor), True))
    return (forward, backward)


def swap_targets(key):
    middle = jax.random.permutation(jax.random.fold_in(key, 61), M - 2 * PB - 2).astype(jnp.int32) + (2 * PB + 1)
    ends = jnp.array([2 * PB, M - 1], dtype=jnp.int32)
    listed = jnp.concatenate([ends, middle[:2 * PB - 2]])
    shuffle = jax.random.permutation(jax.random.fold_in(key, 62), 2 * PB)
    return listed[shuffle].astype(jnp.int32)


def corner_block(key):
    first_block, first_inverse = invertible_pair(key, 71)
    second_block, second_inverse = invertible_pair(key, 81)
    lower_left = residues(jax.random.fold_in(key, 91), (PB, PB))
    upper_right = residues(jax.random.fold_in(key, 92), (PB, PB))
    lower_mult = product_mod(lower_left, first_inverse)
    lower_right = jnp.mod(second_block + product_mod(lower_mult, upper_right), 251).astype(jnp.int32)
    upper_rows = jnp.concatenate([first_block, upper_right], axis=1)
    lower_rows = jnp.concatenate([lower_left, lower_right], axis=1)
    return (jnp.concatenate([upper_rows, lower_rows], axis=0), first_inverse, second_inverse)


def draw_matrix(key, part):
    entries = residues(jax.random.fold_in(key, 11), (M, M))
    corner_parts = corner_block(key)
    targets = swap_targets(key)
    columns = jnp.arange(2 * PB, dtype=jnp.int32)
    entries = entries.at[targets[:, None], columns[None, :]].set(corner_parts[0])
    return entries.astype(jnp.float32).astype(jnp.bfloat16)


def draw_swaps(key, part):
    return swap_targets(key)


def draw_inverse_first(key, part):
    return corner_block(key)[1].astype(jnp.float32).astype(jnp.bfloat16)


def draw_inverse_second(key, part):
    return corner_block(key)[2].astype(jnp.float32).astype(jnp.bfloat16)


def setup_inputs(seed: int = 0) -> dict:
    arg_keys = jax.random.split(jax.random.key(seed), 5)
    matrix = draw_matrix(jax.random.fold_in(arg_keys[4], 71), 0)
    swaps = draw_swaps(jax.random.fold_in(arg_keys[4], 71), 0)
    inverse_first = draw_inverse_first(jax.random.fold_in(arg_keys[4], 71), 0)
    inverse_second = draw_inverse_second(jax.random.fold_in(arg_keys[4], 71), 0)
    return dict(matrix=matrix, swaps=swaps, inverse_first=inverse_first, inverse_second=inverse_second)


def residue(values):
    return jnp.mod(values, 251.0)


def reference(matrix, swaps, inverse_first, inverse_second):
    pair_count = 2 * PB
    targets = swaps.astype(jnp.int32)
    row_order = jnp.arange(M, dtype=jnp.int32)
    row_order = row_order.at[:pair_count].set(targets)
    row_order = row_order.at[targets].set(jnp.arange(pair_count, dtype=jnp.int32))
    permuted = jnp.take(matrix, row_order, axis=0)
    pivot_rows = permuted[:pair_count]
    u_first = pivot_rows[:PB]
    l_top = residue(jnp.dot(pivot_rows[PB:, :PB], inverse_first, preferred_element_type=jnp.float32)).astype(jnp.bfloat16)
    u_second = residue(pivot_rows[PB:].astype(jnp.float32) - jnp.dot(l_top, u_first, preferred_element_type=jnp.float32)).astype(jnp.bfloat16)
    columns = jnp.arange(M, dtype=jnp.int32)
    block_rows = 512
    block_count = M // block_rows

    def one_block(packed):
        row_block, block_start = packed
        row_index = block_start + jnp.arange(block_rows, dtype=jnp.int32)
        l_first = residue(jnp.dot(row_block[:, :PB], inverse_first, preferred_element_type=jnp.float32))
        l_first = jnp.where(row_index[:, None] >= PB, l_first, jnp.zeros_like(l_first)).astype(jnp.bfloat16)
        first_update = residue(row_block.astype(jnp.float32) - jnp.dot(l_first, u_first, preferred_element_type=jnp.float32))
        l_second = residue(jnp.dot(first_update[:, PB:pair_count].astype(jnp.bfloat16), inverse_second, preferred_element_type=jnp.float32))
        l_second = jnp.where(row_index[:, None] >= pair_count, l_second, jnp.zeros_like(l_second)).astype(jnp.bfloat16)
        final_update = residue(first_update - jnp.dot(l_second, u_second, preferred_element_type=jnp.float32))
        multipliers = jnp.pad(jnp.concatenate([l_first, l_second], axis=1).astype(jnp.float32), ((0, 0), (0, M - pair_count)))
        store_mask = ((columns[None, :] < PB) & (row_index[:, None] >= PB)) | ((columns[None, :] >= PB) & (columns[None, :] < pair_count) & (row_index[:, None] >= pair_count))
        stored = jnp.where(store_mask, multipliers, final_update)
        return (stored * (1.0 / 251.0)).astype(jnp.bfloat16)

    blocks = permuted.reshape(block_count, block_rows, M)
    starts = jnp.arange(block_count, dtype=jnp.int32) * block_rows
    return lax.map(one_block, (blocks, starts)).reshape(M, M)
```

```python
import functools

import jax
import jax.numpy as jnp
from jax import lax
from jax.experimental import pallas as pl
from jax.experimental.pallas import tpu as pltpu
from jax.sharding import PartitionSpec as P

modulus = 251.0
scale = 1.0 / 251.0
blocks_axes = ("col", "depth")
f32 = jnp.float32
bf16 = jnp.bfloat16


def dot(a, b):
    return jnp.dot(a, b, preferred_element_type=f32)


def centred(values):
    return values - modulus * jnp.round(values * scale)


def centred_bf16(values):
    return jnp.where(values > 125, values - 251, values).astype(bf16)


def lifted(values):
    return jnp.where(values < 0, values + modulus, values)


def floor_residue(values):
    return values - modulus * jnp.floor((values + 0.5) * scale)


def split_columns(total, parts):
    tiles = total // 128
    edges = [128 * (tiles * k // parts) for k in range(parts + 1)]
    return list(zip(edges[:-1], edges[1:]))


def panel_weights(a, inverse_first, inverse_second, upper, l_top, keep_first, keep_second):
    l_first = centred(dot(a[:, :256], inverse_first))
    if keep_first is not None:
        l_first = jnp.where(keep_first, l_first, 0.0)
    first = l_first.astype(bf16)
    rest = centred(a[:, 256:].astype(f32) - dot(first, upper))
    l_second = centred(dot(rest.astype(bf16), inverse_second))
    if keep_second is not None:
        l_second = jnp.where(keep_second, l_second, 0.0)
    second = l_second.astype(bf16)
    weight_first = centred(l_first - dot(second, l_top)).astype(bf16)
    return l_first, l_second, jnp.concatenate([weight_first, second], axis=1)


def place_kernel(count, spans, step, onehot_ref, *refs):
    parts, out_ref = refs[:-1], refs[-1]
    onehot = onehot_ref[...]
    for t, (lo, hi) in enumerate(spans):
        for c in range(lo, hi, step):
            w = min(step, hi - c)
            stacked = jnp.concatenate(
                [parts[t * count + k][:, c - lo : c - lo + w] for k in range(count)], axis=0
            )
            out_ref[:, c : c + w] = dot(onehot, stacked).astype(bf16)


def place(onehot, parts, spans, count):
    width = spans[-1][1]
    return pl.pallas_call(
        functools.partial(place_kernel, count, spans, 512),
        out_shape=jax.ShapeDtypeStruct((onehot.shape[0], width), bf16),
        compiler_params=pltpu.CompilerParams(vmem_limit_bytes=40 << 20),
        name="place",
    )(onehot, *parts)


def update_kernel(
    base_row, tile, step, has_alias, info, a_ref, m_ref, p_ref, pb_ref, if_ref, is_ref, up_ref, lt_ref, *rest
):
    out_ref = rest[-1]
    tile_row = base_row + pl.program_id(0) * tile
    global_row = info[0] + tile_row
    rows = global_row + lax.broadcasted_iota(jnp.int32, (tile, 1), 0)
    pivots = p_ref.shape[0]
    a = a_ref[...]
    top = base_row < pivots
    in_pivots = (info[0] == 0) & (tile_row < pivots)
    if top:
        start = pl.multiple_of(jnp.minimum(tile_row, pivots - tile), tile)
        window = pl.ds(start, tile)
        a = jnp.where(in_pivots, pb_ref[window, :], a)
    l_first, l_second, weights = panel_weights(
        a, if_ref[...], is_ref[...], up_ref[...], lt_ref[...], rows >= 256, rows >= 512
    )
    width = m_ref.shape[1]
    for c in range(0, width, step):
        m = m_ref[:, c : c + step]
        if top:
            m = jnp.where(in_pivots, p_ref[window, c : c + step], m)
        value = m.astype(f32) - dot(weights, p_ref[:, c : c + step])
        out_ref[:, c : c + step] = (floor_residue(value) * scale).astype(bf16)

    @pl.when(info[1] == 0)
    def _():
        old = out_ref[:, :256]
        out_ref[:, :256] = jnp.where(rows >= 256, (lifted(l_first) * scale).astype(bf16), old)
        old = out_ref[:, 256:512]
        out_ref[:, 256:512] = jnp.where(rows >= 512, (lifted(l_second) * scale).astype(bf16), old)


def update(info, base_row, rows, tile, a, matrix, pivots, small, out):
    height, width = matrix.shape
    step = 512 if width % 512 == 0 else 256
    base = base_row // tile
    whole = lambda x: pl.BlockSpec(x.shape, lambda i, s: (0, 0), pipeline_mode=pl.Buffered(1))
    in_specs = [
        pl.BlockSpec((tile, a.shape[1]), lambda i, s: (i, 0)),
        pl.BlockSpec((tile, width), lambda i, s: (base + i, 0)),
        whole(pivots),
    ] + [whole(x) for x in small]
    operands = [a, matrix, pivots, *small]
    aliases = {}
    if out is not None:
        in_specs.append(pl.BlockSpec(memory_space=pl.ANY))
        operands.append(out)
        aliases = {len(operands): 0}
    return pl.pallas_call(
        functools.partial(update_kernel, base_row, tile, step, out is not None),
        out_shape=jax.ShapeDtypeStruct((height, width), bf16),
        grid_spec=pltpu.PrefetchScalarGridSpec(
            num_scalar_prefetch=1,
            grid=(rows // tile,),
            in_specs=in_specs,
            out_specs=pl.BlockSpec((tile, width), lambda i, s: (base + i, 0)),
        ),
        input_output_aliases=aliases,
        compiler_params=pltpu.CompilerParams(vmem_limit_bytes=48 << 20),
        cost_estimate=pl.CostEstimate(
            flops=2 * rows * 512 * width, bytes_accessed=4 * rows * width, transcendentals=0
        ),
        name="update",
    )(info, *operands)


def merge_kernel(
    spans, info, groups, spread_ref, mask_ref, p_ref, if_ref, is_ref, up_ref, lt_ref, *rest
):
    q_refs = rest[: len(spans)]
    out_in, out_ref, held, fresh, sem_in, sem_out = rest[len(spans) :]
    count = info[2]
    width = p_ref.shape[1]

    def fetch(u):
        source = out_ref.at[pl.ds(pl.multiple_of(groups[u] * 8, 8), 8), :]
        return pltpu.make_async_copy(source, held.at[u], sem_in.at[u])

    def write(u):
        target = out_ref.at[pl.ds(pl.multiple_of(groups[u] * 8, 8), 8), :]
        return pltpu.make_async_copy(held.at[u], target, sem_out.at[u])

    @pl.loop(0, count)
    def _(u):
        fetch(u).start()

    lo, hi = spans[-1]
    a = q_refs[-1][:, width - lo : hi - lo]
    l_first, l_second, weights = panel_weights(
        a, if_ref[...], is_ref[...], up_ref[...], lt_ref[...], None, None
    )
    for k, (lo, hi) in enumerate(spans):
        top = min(hi, width)
        for c in range(lo, top, 512):
            w = min(512, top - c)
            value = q_refs[k][:, c - lo : c - lo + w].astype(f32) - dot(weights, p_ref[:, c : c + w])
            fresh[:, c : c + w] = (floor_residue(value) * scale).astype(bf16)

    @pl.when(info[1] == 0)
    def _():
        fresh[:, :256] = (lifted(l_first) * scale).astype(bf16)
        fresh[:, 256:512] = (lifted(l_second) * scale).astype(bf16)

    @pl.loop(0, count)
    def _(u):
        fetch(u).wait()

    slots = held.shape[0]
    for c in range(0, width, 256):
        spread = dot(spread_ref[...], fresh[:, c : c + 256]).astype(bf16)
        old = held[:, :, c : c + 256].reshape(slots * 8, 256)
        new = jnp.where(mask_ref[...] > 0, spread, old)
        held[:, :, c : c + 256] = new.reshape(slots, 8, 256)

    @pl.loop(0, count)
    def _(u):
        write(u).start()

    @pl.loop(0, count)
    def _(u):
        write(u).wait()


def merge(info, groups, spread, mask, pivots, small, parts, spans, out):
    slots = groups.shape[0]
    width = out.shape[1]
    vmem = pl.BlockSpec(memory_space=pltpu.VMEM)
    anywhere = pl.BlockSpec(memory_space=pl.ANY)
    operands = [spread, mask, pivots, *small, *parts, out]
    return pl.pallas_call(
        functools.partial(merge_kernel, spans),
        out_shape=jax.ShapeDtypeStruct(out.shape, bf16),
        grid_spec=pltpu.PrefetchScalarGridSpec(
            num_scalar_prefetch=2,
            grid=(1,),
            in_specs=[vmem] * (len(operands) - 1) + [anywhere],
            out_specs=anywhere,
            scratch_shapes=[
                pltpu.VMEM((slots, 8, width), bf16),
                pltpu.VMEM((slots, width), bf16),
                pltpu.SemaphoreType.DMA((slots,)),
                pltpu.SemaphoreType.DMA((slots,)),
            ],
        ),
        input_output_aliases={len(operands) + 1: 0},
        compiler_params=pltpu.CompilerParams(vmem_limit_bytes=56 << 20),
        cost_estimate=pl.CostEstimate(
            flops=4 * slots * 512 * width, bytes_accessed=32 * slots * width, transcendentals=0
        ),
        name="merge",
    )(info, groups, *operands)


def local(matrix, swaps, inverse_first, inverse_second):
    height, width = matrix.shape
    panel = inverse_first.shape[0]
    pivots = swaps.shape[0]
    col_count, depth_count, row_count = (
        lax.axis_size("col"), lax.axis_size("depth"), lax.axis_size("row"))
    count = col_count * depth_count
    levels = count.bit_length() - 1
    me = lax.axis_index("col") * depth_count + lax.axis_index("depth")
    row = lax.axis_index("row")
    first_row = me * height
    mean = pivots // count
    slots = -(-(mean + 4 * int(mean**0.5)) // 32) * 32

    def hop(value, bit):
        return lax.ppermute(value, blocks_axes, [(i, i ^ (1 << bit)) for i in range(count)])

    def along_row(value):
        reach = row_count // 2
        while reach:
            pairs = [(i, i + reach) for i in range(0, row_count, 2 * reach)]
            got = lax.ppermute(value, "row", pairs)
            value = jnp.where(row % (2 * reach) == reach, got, value)
            reach //= 2
        return value

    orders = [[(k + s) % levels for k in range(levels)] for s in range(0, levels, -(-levels // 3))]
    spans = split_columns(width, len(orders))
    wide_spans = split_columns(width + pivots, len(orders))

    owner = swaps // height
    index = jnp.arange(pivots, dtype=jnp.int32)
    earlier = (owner[:, None] == owner[None, :]) & (index[None, :] < index[:, None])
    rank = jnp.sum(earlier.astype(jnp.int32), axis=1)
    rounds = jnp.max(rank) // slots + 1
    slot_index = jnp.arange(slots, dtype=jnp.int32)
    all_slots = jnp.arange(count * slots, dtype=jnp.int32)

    def round_slots(turn):
        place_in = rank - turn * slots
        valid = (place_in >= 0) & (place_in < slots)
        mine = (valid & (owner == me))[None, :] & (place_in[None, :] == slot_index[:, None])
        rows = jnp.sum(jnp.where(mine, (swaps - first_row)[None, :], 0), axis=1)
        used = jnp.any(mine, axis=1)
        return place_in, valid, rows, used

    def pivot_exchange(turn):
        place_in, valid, rows, used = round_slots(turn)
        picked = jnp.take(matrix, rows, axis=0, mode="clip")
        picked = centred_bf16(jnp.where(used[:, None], picked, 0))
        key = jnp.where(valid, (owner ^ me) * slots + place_in, -1)
        onehot = (key[:, None] == all_slots[None, :]).astype(bf16)
        head = along_row(picked[:, :pivots])
        for bit in range(levels):
            head = jnp.concatenate([head, hop(head, bit)], axis=0)
        parts = []
        for order, (lo, hi) in zip(orders, spans):
            held = {0: picked[:, lo:hi]}
            for bit in order:
                held.update({mask | (1 << bit): hop(held[mask], bit) for mask in list(held)})
            parts += [held[mask] for mask in range(count)]
        return place(onehot, parts, spans, count), dot(onehot, head).astype(bf16)

    def swapped_out(turn, top_panel):
        place_in, valid, rows, used = round_slots(turn)
        parts = []
        for order, (lo, hi) in zip(orders, wide_spans):
            ordered = sum(((owner >> bit) & 1) << (levels - 1 - k) for k, bit in enumerate(order))
            key = jnp.where(valid, ordered * slots + place_in, -1)
            onehot = (all_slots[:, None] == key[None, :]).astype(bf16)
            source = matrix[:pivots, lo : min(hi, width)]
            if hi > width:
                source = jnp.concatenate([source, top_panel], axis=1)
            value = dot(onehot, source).astype(bf16)
            reached = [0]
            for bit in order:
                half = value.shape[0] // 2
                got = lax.ppermute(
                    value[half:], blocks_axes, [(i, i | (1 << bit)) for i in reached])
                value = jnp.where((me >> bit) & 1 == 1, got, value[:half])
                reached += [i | (1 << bit) for i in reached]
            parts.append(value)
        group = jnp.where(used, rows // 8, -1 - slot_index)
        same = group[:, None] == group[None, :]
        lead = used & ~jnp.any(same & (slot_index[None, :] < slot_index[:, None]), axis=1)
        lead_rank = jnp.sum(lead[None, :] & (slot_index[None, :] < slot_index[:, None]), axis=1)
        at = jnp.sum(jnp.where(same & lead[None, :], lead_rank[None, :], 0), axis=1)
        groups = jnp.sum(
            jnp.where(lead[None, :] & (lead_rank[None, :] == slot_index[:, None]), group[None, :], 0),
            axis=1)
        position = jnp.where(used, at * 8 + rows % 8, -1)
        spread = (jnp.arange(slots * 8)[:, None] == position[None, :]).astype(bf16)
        mask = jnp.max(spread, axis=1, keepdims=True)
        return parts, groups.astype(jnp.int32), jnp.sum(lead.astype(jnp.int32)), spread, mask

    pivot_rows, pivot_head = pivot_exchange(0)

    def more_pivots(state):
        turn, rows_, head_ = state
        extra_rows, extra_head = pivot_exchange(turn)
        return turn + 1, rows_ + extra_rows, head_ + extra_head

    _, pivot_rows, pivot_head = lax.while_loop(
        lambda s: s[0] < rounds, more_pivots, (jnp.int32(1), pivot_rows, pivot_head))

    upper = pivot_head[:panel, panel:]
    l_top = centred(dot(pivot_head[panel:, :panel], inverse_first)).astype(bf16)
    small = [inverse_first, inverse_second, upper, l_top]

    chunks = 5 if height % 5 == 0 else 1
    rows = height // chunks
    tile = 256 if rows % 256 == 0 else 128
    info = jnp.stack([first_row, row, jnp.int32(0)]).astype(jnp.int32)
    out = None
    pieces = []
    for k in range(chunks):
        pieces.append(along_row(matrix[k * rows : (k + 1) * rows, :pivots]))
    for k, piece in enumerate(pieces):
        out = update(info, k * rows, rows, tile, piece, matrix, pivot_rows, [pivot_head, *small], out)

    top_panel = jnp.concatenate(pieces[: -(-pivots // rows)], axis=0)[:pivots]

    def merged(turn, out):
        parts, groups, used, spread, mask = swapped_out(turn, top_panel)
        info = jnp.stack([first_row, row, used]).astype(jnp.int32)
        return merge(info, groups, spread, mask, pivot_rows, small, parts, wide_spans, out)

    out = merged(0, out)
    _, out = lax.while_loop(
        lambda s: s[0] < rounds, lambda s: (s[0] + 1, merged(s[0], s[1])), (jnp.int32(1), out))
    return out


def solution(mesh):
    return jax.shard_map(
        local,
        mesh=mesh,
        in_specs=(P(("col", "depth"), "row"), P(), P(), P()),
        out_specs=P(("col", "depth"), "row"),
        check_vma=False,
    )
```

```python
import functools

import jax
import jax.numpy as jnp
from jax import lax
from jax.experimental import pallas as pl
from jax.experimental.pallas import tpu as pltpu
from jax.sharding import PartitionSpec as P

modulus = 251.0
scale = 1.0 / 251.0
blocks_axes = ("col", "depth")
f32 = jnp.float32
bf16 = jnp.bfloat16


cheap = pl.CostEstimate(flops=0, bytes_accessed=0, transcendentals=0)


def dot(a, b):
    return jnp.dot(a, b, preferred_element_type=f32)


def centred(values):
    return values - modulus * jnp.round(values * scale)


def centred_bf16(values):
    return jnp.where(values > 125, values - 251, values).astype(bf16)


def lifted(values):
    return jnp.where(values < 0, values + modulus, values)


def floor_residue(values):
    return values - modulus * jnp.floor((values + 0.5) * scale)


def split_columns(total, shares):
    tiles = total // 128
    edges = [0]
    for k in range(len(shares)):
        edges.append(128 * round(tiles * sum(shares[: k + 1]) / sum(shares)))
    return list(zip(edges[:-1], edges[1:]))


def panel_weights(a, inverse_first, inverse_second, upper, l_top, keep_first, keep_second):
    l_first = centred(dot(a[:, :256], inverse_first))
    if keep_first is not None:
        l_first = jnp.where(keep_first, l_first, 0.0)
    first = l_first.astype(bf16)
    rest = centred(a[:, 256:].astype(f32) - dot(first, upper))
    l_second = centred(dot(rest.astype(bf16), inverse_second))
    if keep_second is not None:
        l_second = jnp.where(keep_second, l_second, 0.0)
    second = l_second.astype(bf16)
    weight_first = centred(l_first - dot(second, l_top)).astype(bf16)
    return l_first, l_second, jnp.concatenate([weight_first, second], axis=1)


def pick_kernel(spans, rows, lane_ref, matrix_ref, *rest):
    outs, (held, sems) = rest[:-2], rest[-2:]
    slots = held.shape[0]

    def fetch(s):
        source = matrix_ref.at[pl.ds(pl.multiple_of(rows[s] // 8 * 8, 8), 8), :]
        if held.shape[2] < matrix_ref.shape[1]:
            source = source.at[:, 0 : held.shape[2]]
        return pltpu.make_async_copy(source, held.at[s], sems.at[s])

    @pl.loop(0, slots)
    def _(s):
        fetch(s).start()

    slot = lax.broadcasted_iota(jnp.int32, (slots, slots * 8), 0)
    place = lax.broadcasted_iota(jnp.int32, (slots, slots * 8), 1)
    select = (place == slot * 8 + lane_ref[...]) & (lane_ref[...] >= 0)
    select = select.astype(f32).astype(bf16)

    @pl.loop(0, slots)
    def _(s):
        fetch(s).wait()

    for t, (lo, hi) in enumerate(spans):
        for c in range(lo, hi, 256):
            w = min(256, hi - c)
            value = dot(select, held[:, :, c : c + w].reshape(slots * 8, w))
            value = jnp.where(value > 125.0, value - modulus, value).astype(bf16)
            outs[t][:, c - lo : c - lo + w] = value


def pick(rows, lane, matrix, spans):
    slots = rows.shape[0]
    vmem = pl.BlockSpec(memory_space=pltpu.VMEM)
    return pl.pallas_call(
        functools.partial(pick_kernel, spans),
        out_shape=[jax.ShapeDtypeStruct((slots, hi - lo), bf16) for lo, hi in spans],
        grid_spec=pltpu.PrefetchScalarGridSpec(
            num_scalar_prefetch=1,
            grid=(1,),
            in_specs=[vmem, pl.BlockSpec(memory_space=pl.ANY)],
            out_specs=[vmem] * len(spans),
            scratch_shapes=[
                pltpu.VMEM((slots, 8, spans[-1][1]), bf16),
                pltpu.SemaphoreType.DMA((slots,)),
            ],
        ),
        compiler_params=pltpu.CompilerParams(vmem_limit_bytes=32 << 20),
        cost_estimate=cheap,
        name="pick",
    )(rows, lane, matrix)


def source_kernel(span, width, counts, info, key_ref, *refs):
    refs, (held, sem) = refs[:-2], refs[-2:]
    inputs, outs = refs[: -len(counts)], refs[-len(counts) :]
    lo, hi = span
    top = min(hi, width)
    total = sum(counts)

    @pl.when(info[0] == 0)
    def _():
        pivots = key_ref.shape[1]
        fetch = pltpu.make_async_copy(inputs[0].at[0:pivots, lo:top], held, sem)
        fetch.start()
        place = lax.broadcasted_iota(jnp.int32, (total, pivots), 0)
        onehot = (place == key_ref[...]).astype(f32).astype(bf16)
        fetch.wait()
        pieces = [(held, c - lo, c - lo, min(512, top - c)) for c in range(lo, top, 512)]
        pieces += [(inputs[-1], c - width, c - lo, min(512, hi - c)) for c in range(width, hi, 512)]
        for ref, start, c, w in pieces:
            value = dot(onehot, ref[:, start : start + w]).astype(bf16)
            at = 0
            for k, n in enumerate(counts):
                outs[k][:, c : c + w] = value[at : at + n]
                at += n


def source(info, key, panel, matrix, span, counts):
    pivots = key.shape[1]
    width = matrix.shape[1]
    lo, hi = span
    vmem = pl.BlockSpec(memory_space=pltpu.VMEM)
    operands = [matrix] if hi <= width else [matrix, panel]
    return pl.pallas_call(
        functools.partial(source_kernel, span, width, counts),
        out_shape=[jax.ShapeDtypeStruct((n, hi - lo), bf16) for n in counts],
        grid_spec=pltpu.PrefetchScalarGridSpec(
            num_scalar_prefetch=1,
            grid=(1,),
            in_specs=[vmem, pl.BlockSpec(memory_space=pl.ANY)] + [vmem] * (len(operands) - 1),
            out_specs=[vmem] * len(counts),
            scratch_shapes=[
                pltpu.VMEM((pivots, min(hi, width) - lo), bf16),
                pltpu.SemaphoreType.DMA,
            ],
        ),
        compiler_params=pltpu.CompilerParams(vmem_limit_bytes=40 << 20),
        cost_estimate=cheap,
        name="source",
    )(info, key, *operands)


def place_kernel(spans, per, key_ref, *refs):
    parts, out_ref = refs[:-1], refs[-1]
    pivots = out_ref.shape[0]
    total = sum(parts[k].shape[0] for k in range(per))
    place = lax.broadcasted_iota(jnp.int32, (pivots, total), 1)
    for t, (lo, hi) in enumerate(spans):
        onehot = (place == key_ref[:, t : t + 1]).astype(f32).astype(bf16)
        for c in range(lo, hi, 512):
            w = min(512, hi - c)
            stacked = jnp.concatenate(
                [parts[t * per + k][:, c - lo : c - lo + w] for k in range(per)], axis=0
            )
            out_ref[:, c : c + w] = dot(onehot, stacked).astype(bf16)


def place(keys, parts, spans):
    width = spans[-1][1]
    return pl.pallas_call(
        functools.partial(place_kernel, spans, len(parts) // len(spans)),
        out_shape=jax.ShapeDtypeStruct((keys.shape[0], width), bf16),
        compiler_params=pltpu.CompilerParams(vmem_limit_bytes=40 << 20),
        cost_estimate=cheap,
        name="place",
    )(keys, *parts)


def weights_kernel(
    base_row, tile, info, a_ref, pb_ref, if_ref, is_ref, up_ref, lt_ref, w_ref, head_ref
):
    tile_row = base_row + pl.program_id(0) * tile
    rows = info[0] + tile_row + lax.broadcasted_iota(jnp.int32, (tile, 1), 0)
    pivots = pb_ref.shape[0]
    a = a_ref[...]
    if base_row < pivots:
        start = pl.multiple_of(jnp.minimum(tile_row, pivots - tile), tile)
        a = jnp.where((info[0] == 0) & (tile_row < pivots), pb_ref[pl.ds(start, tile), :], a)
    l_first, l_second, weights = panel_weights(
        a, if_ref[...], is_ref[...], up_ref[...], lt_ref[...], rows >= 256, rows >= 512
    )
    w_ref[...] = weights
    head_ref[:, :256] = (lifted(l_first) * scale).astype(bf16)
    head_ref[:, 256:] = (lifted(l_second) * scale).astype(bf16)


def weights_of(info, base_row, tile, a, small):
    rows, pivots = a.shape
    whole = lambda x: pl.BlockSpec(x.shape, lambda i, s: (0, 0))
    block = pl.BlockSpec((tile, pivots), lambda i, s: (i, 0))
    return pl.pallas_call(
        functools.partial(weights_kernel, base_row, tile),
        out_shape=[jax.ShapeDtypeStruct((rows, pivots), bf16)] * 2,
        grid_spec=pltpu.PrefetchScalarGridSpec(
            num_scalar_prefetch=1,
            grid=(rows // tile,),
            in_specs=[block] + [whole(x) for x in small],
            out_specs=[block] * 2,
        ),
        compiler_params=pltpu.CompilerParams(vmem_limit_bytes=24 << 20),
        cost_estimate=cheap,
        name="weights",
    )(info, a, *small)


def update_kernel(base_row, tile, step, info, mark_in, w_ref, head_ref, m_ref, p_ref, *rest):
    out_ref, mark_ref = rest[-2:]
    mark_ref[...] = mark_in[...]
    tile_row = base_row + pl.program_id(0) * tile
    rows = info[0] + tile_row + lax.broadcasted_iota(jnp.int32, (tile, 1), 0)
    pivots = p_ref.shape[0]
    weights = w_ref[...]
    top = base_row < pivots
    in_pivots = (info[0] == 0) & (tile_row < pivots)
    if top:
        start = pl.multiple_of(jnp.minimum(tile_row, pivots - tile), tile)
        window = pl.ds(start, tile)
    width = m_ref.shape[1]
    for c in range(0, width, step):
        m = m_ref[:, c : c + step]
        if top:
            m = jnp.where(in_pivots, p_ref[window, c : c + step], m)
        value = m.astype(f32) - dot(weights, p_ref[:, c : c + step])
        out_ref[:, c : c + step] = (floor_residue(value) * scale).astype(bf16)

    @pl.when(info[1] == 0)
    def _():
        for lo in (0, 256):
            old = out_ref[:, lo : lo + 256]
            keep = rows >= lo + 256
            out_ref[:, lo : lo + 256] = jnp.where(keep, head_ref[:, lo : lo + 256], old)


def update(info, mark, base_row, rows, tile, weights, head, matrix, pivots, out):
    height, width = matrix.shape
    step = 512 if width % 512 == 0 else 256
    base = base_row // tile
    in_specs = [
        pl.BlockSpec((8, 128), lambda i, s: (0, 0)),
        pl.BlockSpec((tile, weights.shape[1]), lambda i, s: (base + i, 0)),
        pl.BlockSpec((tile, weights.shape[1]), lambda i, s: (base + i, 0)),
        pl.BlockSpec((tile, width), lambda i, s: (base + i, 0)),
        pl.BlockSpec(pivots.shape, lambda i, s: (0, 0), pipeline_mode=pl.Buffered(1)),
    ]
    operands = [mark, weights, head, matrix, pivots]
    aliases = {}
    if out is not None:
        in_specs.append(pl.BlockSpec(memory_space=pl.ANY))
        operands.append(out)
        aliases = {len(operands): 0}
    return pl.pallas_call(
        functools.partial(update_kernel, base_row, tile, step),
        out_shape=[
            jax.ShapeDtypeStruct((height, width), bf16),
            jax.ShapeDtypeStruct((8, 128), f32),
        ],
        grid_spec=pltpu.PrefetchScalarGridSpec(
            num_scalar_prefetch=1,
            grid=(rows // tile,),
            in_specs=in_specs,
            out_specs=[
                pl.BlockSpec((tile, width), lambda i, s: (base + i, 0)),
                pl.BlockSpec((8, 128), lambda i, s: (0, 0)),
            ],
        ),
        input_output_aliases=aliases,
        compiler_params=pltpu.CompilerParams(vmem_limit_bytes=48 << 20),
        cost_estimate=pl.CostEstimate(
            flops=8 * rows * 512 * width, bytes_accessed=16 * rows * width, transcendentals=0
        ),
        name="update",
    )(info, *operands)


def merge_kernel(
    spans, info, groups, spread_ref, mask_ref, p_ref, if_ref, is_ref, up_ref, lt_ref, *rest
):
    q_refs = rest[: len(spans)]
    out_in, out_ref, held, fresh, sem_in, sem_out = rest[len(spans) :]
    count = info[2]
    width = p_ref.shape[1]

    def fetch(u):
        source = out_ref.at[pl.ds(pl.multiple_of(groups[u] * 8, 8), 8), :]
        return pltpu.make_async_copy(source, held.at[u], sem_in.at[u])

    def write(u):
        target = out_ref.at[pl.ds(pl.multiple_of(groups[u] * 8, 8), 8), :]
        return pltpu.make_async_copy(held.at[u], target, sem_out.at[u])

    @pl.loop(0, count)
    def _(u):
        fetch(u).start()

    lo, hi = spans[-1]
    a = q_refs[-1][:, width - lo : hi - lo]
    l_first, l_second, weights = panel_weights(
        a, if_ref[...], is_ref[...], up_ref[...], lt_ref[...], None, None
    )
    for k, (lo, hi) in enumerate(spans):
        top = min(hi, width)
        for c in range(lo, top, 512):
            w = min(512, top - c)
            value = q_refs[k][:, c - lo : c - lo + w].astype(f32) - dot(weights, p_ref[:, c : c + w])
            fresh[:, c : c + w] = (floor_residue(value) * scale).astype(bf16)

    @pl.when(info[1] == 0)
    def _():
        fresh[:, :256] = (lifted(l_first) * scale).astype(bf16)
        fresh[:, 256:512] = (lifted(l_second) * scale).astype(bf16)

    @pl.loop(0, count)
    def _(u):
        fetch(u).wait()

    slots = held.shape[0]
    for c in range(0, width, 256):
        spread = dot(spread_ref[...], fresh[:, c : c + 256]).astype(bf16)
        old = held[:, :, c : c + 256].reshape(slots * 8, 256)
        new = jnp.where(mask_ref[...] > 0, spread, old)
        held[:, :, c : c + 256] = new.reshape(slots, 8, 256)

    @pl.loop(0, count)
    def _(u):
        write(u).start()

    @pl.loop(0, count)
    def _(u):
        write(u).wait()


def merge(info, groups, spread, mask, pivots, small, parts, spans, out):
    slots = groups.shape[0]
    width = out.shape[1]
    vmem = pl.BlockSpec(memory_space=pltpu.VMEM)
    anywhere = pl.BlockSpec(memory_space=pl.ANY)
    operands = [spread, mask, pivots, *small, *parts, out]
    return pl.pallas_call(
        functools.partial(merge_kernel, spans),
        out_shape=jax.ShapeDtypeStruct(out.shape, bf16),
        grid_spec=pltpu.PrefetchScalarGridSpec(
            num_scalar_prefetch=2,
            grid=(1,),
            in_specs=[vmem] * (len(operands) - 1) + [anywhere],
            out_specs=anywhere,
            scratch_shapes=[
                pltpu.VMEM((slots, 8, width), bf16),
                pltpu.VMEM((slots, width), bf16),
                pltpu.SemaphoreType.DMA((slots,)),
                pltpu.SemaphoreType.DMA((slots,)),
            ],
        ),
        input_output_aliases={len(operands) + 1: 0},
        compiler_params=pltpu.CompilerParams(vmem_limit_bytes=56 << 20),
        cost_estimate=cheap,
        name="merge",
    )(info, groups, *operands)


def local(matrix, swaps, inverse_first, inverse_second):
    height, width = matrix.shape
    panel = inverse_first.shape[0]
    pivots = swaps.shape[0]
    col_count, depth_count, row_count = (
        lax.axis_size("col"), lax.axis_size("depth"), lax.axis_size("row"))
    count = col_count * depth_count
    levels = count.bit_length() - 1
    me = lax.axis_index("col") * depth_count + lax.axis_index("depth")
    row = lax.axis_index("row")
    first_row = me * height
    mean = pivots // count
    slots = -(-(mean + 4 * int(mean**0.5)) // 32) * 32

    def hop(value, bit):
        return lax.ppermute(value, blocks_axes, [(i, i ^ (1 << bit)) for i in range(count)])

    reaches = []
    while row_count >> (len(reaches) + 1):
        reaches.append(row_count >> (len(reaches) + 1))

    def row_hop(value, reach):
        pairs = [(i, i + reach) for i in range(0, row_count, 2 * reach)]
        got = lax.ppermute(value, "row", pairs)
        return jnp.where(row % (2 * reach) == reach, got, value)

    def along_row(value):
        for reach in reaches:
            value = row_hop(value, reach)
        return value

    together = lax.optimization_barrier

    orders = [[(k + s) % levels for k in range(levels)] for s in range(0, levels, -(-levels // 3))]
    spans = split_columns(width, [0.38, 0.28, 0.34])
    wide_spans = split_columns(width + pivots, [0.32, 0.34, 0.34])
    counts = [slots] + [slots << k for k in range(levels)]

    owner = swaps // height
    index = jnp.arange(pivots, dtype=jnp.int32)
    earlier = (owner[:, None] == owner[None, :]) & (index[None, :] < index[:, None])
    rank = jnp.sum(earlier.astype(jnp.int32), axis=1)
    rounds = jnp.max(rank) // slots + 1
    slot_index = jnp.arange(slots, dtype=jnp.int32)
    all_slots = jnp.arange(count * slots, dtype=jnp.int32)

    def round_slots(turn):
        place_in = rank - turn * slots
        valid = (place_in >= 0) & (place_in < slots)
        mine = (valid & (owner == me))[None, :] & (place_in[None, :] == slot_index[:, None])
        rows = jnp.sum(jnp.where(mine, (swaps - first_row)[None, :], 0), axis=1)
        used = jnp.any(mine, axis=1)
        return place_in, valid, rows, used

    def pivot_start(turn):
        place_in, valid, rows, used = round_slots(turn)
        lane = jnp.where(used, rows % 8, -1)[:, None]
        picked = pick(rows, lane, matrix, spans)
        relative = owner ^ me

        def key_of(order):
            ordered = sum(((relative >> bit) & 1) << k for k, bit in enumerate(order))
            return jnp.where(valid, ordered * slots + place_in, -1)

        keys = jnp.stack([key_of(order) for order in orders], axis=1)
        head_onehot = (key_of(range(levels))[:, None] == all_slots[None, :]).astype(bf16)
        return [[part] for part in picked], keys, head_onehot

    def join(pieces):
        return [held[0] if len(held) == 1 else jnp.concatenate(held, axis=0) for held in pieces]

    def pivot_hop(pieces, joined, level):
        return [
            held + [hop(part, order[level])] for held, part, order in zip(pieces, joined, orders)
        ]

    def head_hops(part):
        head = along_row(part)
        for level in range(levels):
            head = jnp.concatenate([head, hop(head, level)], axis=0)
        return head

    def flat(nested):
        return [value for held in nested for value in held]

    def swap_slabs(turn, top_panel):
        place_in, valid, _, _ = round_slots(turn)
        keys = []
        for order in orders:
            ordered = sum(((owner >> bit) & 1) << (levels - 1 - k) for k, bit in enumerate(order))
            keys.append(jnp.where(valid, ordered * slots + place_in, -1))
        at = jnp.stack([first_row])
        return [
            source(at, key[None, :], top_panel, matrix, span, counts)
            for key, span in zip(keys, wide_spans)
        ]

    def swap_hop(slabs, level):
        result = []
        for order, (own, *leaving) in zip(orders, slabs):
            bit = order[level]
            reached = [0]
            for done in order[:level]:
                reached += [i | (1 << done) for i in reached]
            got = lax.ppermute(leaving[-1], blocks_axes, [(i, i | (1 << bit)) for i in reached])
            took = (me >> bit) & 1 == 1
            kept = [
                jnp.where(took, got[(slots << k) : (slots << (k + 1))], leaving[k])
                for k in range(levels - 1 - level)
            ]
            result.append([jnp.where(took, got[:slots], own), *kept])
        return result

    def swap_tables(turn):
        _, _, rows, used = round_slots(turn)
        group = jnp.where(used, rows // 8, -1 - slot_index)
        same = group[:, None] == group[None, :]
        before = slot_index[None, :] < slot_index[:, None]
        lead = used & ~jnp.any(same & before, axis=1)
        lead_rank = jnp.sum((lead[None, :] & before).astype(jnp.int32), axis=1)
        at = jnp.sum(jnp.where(same & lead[None, :], lead_rank[None, :], 0), axis=1)
        chosen = lead[None, :] & (lead_rank[None, :] == slot_index[:, None])
        groups = jnp.sum(jnp.where(chosen, group[None, :], 0), axis=1)
        position = jnp.where(used, at * 8 + rows % 8, -1)
        spread = (jnp.arange(slots * 8)[:, None] == position[None, :]).astype(bf16)
        mask = jnp.max(spread, axis=1, keepdims=True)
        return groups, jnp.sum(lead.astype(jnp.int32)), spread, mask

    tile = 256 if height % 1280 == 0 else 128
    def panel_hops(lo, hi, *after):
        value = matrix[lo:hi, :pivots]
        far = row_hop(tie(value, *after) if after else value, reaches[0])
        near = far
        for reach in reaches[1:]:
            near = row_hop(near, reach)
        return far, near

    def near_of(value):
        for reach in reaches[1:]:
            value = row_hop(value, reach)
        return value

    middle = max(pivots, height * 2 // 5 // 128 * 128)
    first_far = row_hop(matrix[:middle, :pivots], reaches[0])
    second, first_far = together((matrix[middle:, :pivots], first_far))
    second_far = row_hop(second, reaches[0])
    pieces, keys, head_onehot = pivot_start(0)
    head_part = pieces[0][0][:, :pivots]
    for level in range(levels - 1):
        pieces = pivot_hop(pieces, join(pieces), level)
    joined, first_far = together((join(pieces), first_far))
    first_near = near_of(first_far)
    slabs = swap_slabs(0, first_near[:pivots])
    pieces = pivot_hop(pieces, joined, levels - 1)
    pieces, second_far, slabs = together((pieces, second_far, slabs))
    second_near = near_of(second_far)
    slabs = swap_hop(slabs, 0)
    pivot_rows = place(keys, flat(pieces), spans)
    pivot_head = dot(head_onehot, head_hops(head_part)).astype(bf16)

    def more_pivots(state):
        turn, rows_, head_ = state
        pieces, keys, head_onehot = pivot_start(turn)
        for level in range(levels):
            pieces = pivot_hop(pieces, join(pieces), level)
        extra_head = dot(head_onehot, head_hops(pieces[0][0][:, :pivots])).astype(bf16)
        return turn + 1, rows_ + place(keys, flat(pieces), spans), head_ + extra_head

    _, pivot_rows, pivot_head = lax.while_loop(
        lambda s: s[0] < rounds, more_pivots, (jnp.int32(1), pivot_rows, pivot_head))

    upper = pivot_head[:panel, panel:]
    l_top = centred(dot(pivot_head[panel:, :panel], inverse_first)).astype(bf16)
    small = [inverse_first, inverse_second, upper, l_top]
    info = jnp.stack([first_row, row]).astype(jnp.int32)
    panel_all = jnp.concatenate([first_near, second_near], axis=0)
    weights, head = weights_of(info, 0, tile, panel_all, [pivot_head, *small])
    cuts = [height * k // 5 // tile * tile for k in (0, 2, 4, 5)]
    mark = jnp.zeros((8, 128), f32)
    out = None
    for k, (lo, hi) in enumerate(zip(cuts[:-1], cuts[1:])):
        out, mark = update(info, mark, lo, hi - lo, tile, weights, head, matrix, pivot_rows, out)
        if k + 1 < min(levels, 3):
            slabs, mark = together((slabs, mark))
            slabs = swap_hop(slabs, k + 1)
    for level in range(3, levels):
        slabs = swap_hop(slabs, level)

    def merged(turn, out, slabs, mark):
        parts = [own[0] for own in slabs]
        groups, used, spread, mask = swap_tables(turn)
        info = jnp.stack([first_row, row, used + mark[0, 0].astype(jnp.int32)]).astype(jnp.int32)
        return merge(info, groups, spread, mask, pivot_rows, small, parts, wide_spans, out)

    out = merged(0, out, slabs, mark)

    def more_swapped(state):
        turn, out = state
        slabs = swap_slabs(turn, first_near[:pivots])
        for level in range(levels):
            slabs = swap_hop(slabs, level)
        return turn + 1, merged(turn, out, slabs, mark)

    _, out = lax.while_loop(lambda s: s[0] < rounds, more_swapped, (jnp.int32(1), out))
    return out


def solution(mesh):
    return jax.shard_map(
        local,
        mesh=mesh,
        in_specs=(P(("col", "depth"), "row"), P(), P(), P()),
        out_specs=P(("col", "depth"), "row"),
        check_vma=False,
    )
```

```python
import functools

import jax
import jax.numpy as jnp
from jax import lax
from jax.experimental import pallas as pl
from jax.experimental.pallas import tpu as pltpu
from jax.sharding import PartitionSpec as P

modulus = 251.0
scale = 1.0 / 251.0
blocks_axes = ("col", "depth")
f32 = jnp.float32
bf16 = jnp.bfloat16


cheap = pl.CostEstimate(flops=0, bytes_accessed=0, transcendentals=0)


def dot(a, b):
    return jnp.dot(a, b, preferred_element_type=f32)


def centred(values):
    return values - modulus * jnp.round(values * scale)


def centred_bf16(values):
    return jnp.where(values > 125, values - 251, values).astype(bf16)


def lifted(values):
    return jnp.where(values < 0, values + modulus, values)


def floor_residue(values):
    return values - modulus * jnp.floor((values + 0.5) * scale)


def split_columns(total, shares):
    tiles = total // 128
    edges = [0]
    for k in range(len(shares)):
        edges.append(128 * round(tiles * sum(shares[: k + 1]) / sum(shares)))
    return list(zip(edges[:-1], edges[1:]))


def panel_weights(a, inverse_first, inverse_second, upper, l_top, keep_first, keep_second):
    l_first = centred(dot(a[:, :256], inverse_first))
    if keep_first is not None:
        l_first = jnp.where(keep_first, l_first, 0.0)
    first = l_first.astype(bf16)
    rest = centred(a[:, 256:].astype(f32) - dot(first, upper))
    l_second = centred(dot(rest.astype(bf16), inverse_second))
    if keep_second is not None:
        l_second = jnp.where(keep_second, l_second, 0.0)
    second = l_second.astype(bf16)
    weight_first = centred(l_first - dot(second, l_top)).astype(bf16)
    return l_first, l_second, jnp.concatenate([weight_first, second], axis=1)


def pick_kernel(spans, rows, lane_ref, matrix_ref, *rest):
    outs, (held, sems) = rest[:-2], rest[-2:]
    slots = held.shape[0]

    def fetch(s):
        source = matrix_ref.at[pl.ds(pl.multiple_of(rows[s] // 8 * 8, 8), 8), :]
        if held.shape[2] < matrix_ref.shape[1]:
            source = source.at[:, 0 : held.shape[2]]
        return pltpu.make_async_copy(source, held.at[s], sems.at[s])

    @pl.loop(0, slots)
    def _(s):
        fetch(s).start()

    slot = lax.broadcasted_iota(jnp.int32, (slots, slots * 8), 0)
    place = lax.broadcasted_iota(jnp.int32, (slots, slots * 8), 1)
    select = (place == slot * 8 + lane_ref[...]) & (lane_ref[...] >= 0)
    select = select.astype(f32).astype(bf16)

    @pl.loop(0, slots)
    def _(s):
        fetch(s).wait()

    for t, (lo, hi) in enumerate(spans):
        for c in range(lo, hi, 256):
            w = min(256, hi - c)
            value = dot(select, held[:, :, c : c + w].reshape(slots * 8, w))
            value = jnp.where(value > 125.0, value - modulus, value).astype(bf16)
            outs[t][:, c - lo : c - lo + w] = value


def pick(rows, lane, matrix, spans):
    slots = rows.shape[0]
    vmem = pl.BlockSpec(memory_space=pltpu.VMEM)
    return pl.pallas_call(
        functools.partial(pick_kernel, spans),
        out_shape=[jax.ShapeDtypeStruct((slots, hi - lo), bf16) for lo, hi in spans],
        grid_spec=pltpu.PrefetchScalarGridSpec(
            num_scalar_prefetch=1,
            grid=(1,),
            in_specs=[vmem, pl.BlockSpec(memory_space=pl.ANY)],
            out_specs=[vmem] * len(spans),
            scratch_shapes=[
                pltpu.VMEM((slots, 8, spans[-1][1]), bf16),
                pltpu.SemaphoreType.DMA((slots,)),
            ],
        ),
        compiler_params=pltpu.CompilerParams(vmem_limit_bytes=32 << 20),
        cost_estimate=cheap,
        name="pick",
    )(rows, lane, matrix)


def source_kernel(span, width, counts, info, key_ref, *refs):
    refs, (held, sem) = refs[:-2], refs[-2:]
    inputs, outs = refs[: -len(counts)], refs[-len(counts) :]
    lo, hi = span
    top = min(hi, width)
    total = sum(counts)

    @pl.when(info[0] == 0)
    def _():
        pivots = key_ref.shape[1]
        fetch = pltpu.make_async_copy(inputs[0].at[0:pivots, lo:top], held, sem)
        fetch.start()
        place = lax.broadcasted_iota(jnp.int32, (total, pivots), 0)
        onehot = (place == key_ref[...]).astype(f32).astype(bf16)
        fetch.wait()
        pieces = [(held, c - lo, c - lo, min(512, top - c)) for c in range(lo, top, 512)]
        pieces += [(inputs[-1], c - width, c - lo, min(512, hi - c)) for c in range(width, hi, 512)]
        for ref, start, c, w in pieces:
            value = dot(onehot, ref[:, start : start + w]).astype(bf16)
            at = 0
            for k, n in enumerate(counts):
                outs[k][:, c : c + w] = value[at : at + n]
                at += n


def source(info, key, panel, matrix, span, counts):
    pivots = key.shape[1]
    width = matrix.shape[1]
    lo, hi = span
    vmem = pl.BlockSpec(memory_space=pltpu.VMEM)
    operands = [matrix] if hi <= width else [matrix, panel]
    return pl.pallas_call(
        functools.partial(source_kernel, span, width, counts),
        out_shape=[jax.ShapeDtypeStruct((n, hi - lo), bf16) for n in counts],
        grid_spec=pltpu.PrefetchScalarGridSpec(
            num_scalar_prefetch=1,
            grid=(1,),
            in_specs=[vmem, pl.BlockSpec(memory_space=pl.ANY)] + [vmem] * (len(operands) - 1),
            out_specs=[vmem] * len(counts),
            scratch_shapes=[
                pltpu.VMEM((pivots, min(hi, width) - lo), bf16),
                pltpu.SemaphoreType.DMA,
            ],
        ),
        compiler_params=pltpu.CompilerParams(vmem_limit_bytes=40 << 20),
        cost_estimate=cheap,
        name="source",
    )(info, key, *operands)


def place_kernel(spans, per, key_ref, *refs):
    parts, out_ref = refs[:-1], refs[-1]
    pivots = out_ref.shape[0]
    total = sum(parts[k].shape[0] for k in range(per))
    place = lax.broadcasted_iota(jnp.int32, (pivots, total), 1)
    for t, (lo, hi) in enumerate(spans):
        onehot = (place == key_ref[:, t : t + 1]).astype(f32).astype(bf16)
        for c in range(lo, hi, 512):
            w = min(512, hi - c)
            stacked = jnp.concatenate(
                [parts[t * per + k][:, c - lo : c - lo + w] for k in range(per)], axis=0
            )
            out_ref[:, c : c + w] = dot(onehot, stacked).astype(bf16)


def place(keys, parts, spans):
    width = spans[-1][1]
    return pl.pallas_call(
        functools.partial(place_kernel, spans, len(parts) // len(spans)),
        out_shape=jax.ShapeDtypeStruct((keys.shape[0], width), bf16),
        compiler_params=pltpu.CompilerParams(vmem_limit_bytes=40 << 20),
        cost_estimate=cheap,
        name="place",
    )(keys, *parts)


def weights_kernel(
    base_row, tile, info, a_ref, pb_ref, if_ref, is_ref, up_ref, lt_ref, w_ref, head_ref
):
    tile_row = base_row + pl.program_id(0) * tile
    rows = info[0] + tile_row + lax.broadcasted_iota(jnp.int32, (tile, 1), 0)
    pivots = pb_ref.shape[0]
    a = a_ref[...]
    if base_row < pivots:
        start = pl.multiple_of(jnp.minimum(tile_row, pivots - tile), tile)
        a = jnp.where((info[0] == 0) & (tile_row < pivots), pb_ref[pl.ds(start, tile), :], a)
    l_first, l_second, weights = panel_weights(
        a, if_ref[...], is_ref[...], up_ref[...], lt_ref[...], rows >= 256, rows >= 512
    )
    w_ref[...] = weights
    head_ref[:, :256] = (lifted(l_first) * scale).astype(bf16)
    head_ref[:, 256:] = (lifted(l_second) * scale).astype(bf16)


def weights_of(info, base_row, tile, a, small):
    rows, pivots = a.shape
    whole = lambda x: pl.BlockSpec(x.shape, lambda i, s: (0, 0))
    block = pl.BlockSpec((tile, pivots), lambda i, s: (i, 0))
    return pl.pallas_call(
        functools.partial(weights_kernel, base_row, tile),
        out_shape=[jax.ShapeDtypeStruct((rows, pivots), bf16)] * 2,
        grid_spec=pltpu.PrefetchScalarGridSpec(
            num_scalar_prefetch=1,
            grid=(rows // tile,),
            in_specs=[block] + [whole(x) for x in small],
            out_specs=[block] * 2,
        ),
        compiler_params=pltpu.CompilerParams(vmem_limit_bytes=24 << 20),
        cost_estimate=cheap,
        name="weights",
    )(info, a, *small)


def update_kernel(base_row, tile, step, info, mark_in, w_ref, head_ref, m_ref, p_ref, *rest):
    out_ref, mark_ref = rest[-2:]
    mark_ref[...] = mark_in[...]
    tile_row = base_row + pl.program_id(0) * tile
    rows = info[0] + tile_row + lax.broadcasted_iota(jnp.int32, (tile, 1), 0)
    pivots = p_ref.shape[0]
    weights = w_ref[...]
    top = base_row < pivots
    in_pivots = (info[0] == 0) & (tile_row < pivots)
    if top:
        start = pl.multiple_of(jnp.minimum(tile_row, pivots - tile), tile)
        window = pl.ds(start, tile)
    width = m_ref.shape[1]
    for c in range(0, width, step):
        m = m_ref[:, c : c + step]
        if top:
            m = jnp.where(in_pivots, p_ref[window, c : c + step], m)
        value = m.astype(f32) - dot(weights, p_ref[:, c : c + step])
        out_ref[:, c : c + step] = (floor_residue(value) * scale).astype(bf16)

    @pl.when(info[1] == 0)
    def _():
        for lo in (0, 256):
            old = out_ref[:, lo : lo + 256]
            keep = rows >= lo + 256
            out_ref[:, lo : lo + 256] = jnp.where(keep, head_ref[:, lo : lo + 256], old)


def update(info, mark, base_row, rows, tile, weights, head, matrix, pivots, out):
    height, width = matrix.shape
    step = 512 if width % 512 == 0 else 256
    base = base_row // tile
    in_specs = [
        pl.BlockSpec((8, 128), lambda i, s: (0, 0)),
        pl.BlockSpec((tile, weights.shape[1]), lambda i, s: (base + i, 0)),
        pl.BlockSpec((tile, weights.shape[1]), lambda i, s: (base + i, 0)),
        pl.BlockSpec((tile, width), lambda i, s: (base + i, 0)),
        pl.BlockSpec(pivots.shape, lambda i, s: (0, 0), pipeline_mode=pl.Buffered(1)),
    ]
    operands = [mark, weights, head, matrix, pivots]
    aliases = {}
    if out is not None:
        in_specs.append(pl.BlockSpec(memory_space=pl.ANY))
        operands.append(out)
        aliases = {len(operands): 0}
    return pl.pallas_call(
        functools.partial(update_kernel, base_row, tile, step),
        out_shape=[
            jax.ShapeDtypeStruct((height, width), bf16),
            jax.ShapeDtypeStruct((8, 128), f32),
        ],
        grid_spec=pltpu.PrefetchScalarGridSpec(
            num_scalar_prefetch=1,
            grid=(rows // tile,),
            in_specs=in_specs,
            out_specs=[
                pl.BlockSpec((tile, width), lambda i, s: (base + i, 0)),
                pl.BlockSpec((8, 128), lambda i, s: (0, 0)),
            ],
        ),
        input_output_aliases=aliases,
        compiler_params=pltpu.CompilerParams(vmem_limit_bytes=48 << 20),
        cost_estimate=pl.CostEstimate(
            flops=8 * rows * 512 * width, bytes_accessed=16 * rows * width, transcendentals=0
        ),
        name="update",
    )(info, *operands)


def merge_kernel(
    spans, info, groups, spread_ref, mask_ref, p_ref, if_ref, is_ref, up_ref, lt_ref, *rest
):
    q_refs = rest[: len(spans)]
    out_in, out_ref, held, fresh, sem_in, sem_out = rest[len(spans) :]
    count = info[2]
    width = p_ref.shape[1]

    def fetch(u):
        source = out_ref.at[pl.ds(pl.multiple_of(groups[u] * 8, 8), 8), :]
        return pltpu.make_async_copy(source, held.at[u], sem_in.at[u])

    def write(u):
        target = out_ref.at[pl.ds(pl.multiple_of(groups[u] * 8, 8), 8), :]
        return pltpu.make_async_copy(held.at[u], target, sem_out.at[u])

    @pl.loop(0, count)
    def _(u):
        fetch(u).start()

    lo, hi = spans[-1]
    a = q_refs[-1][:, width - lo : hi - lo]
    l_first, l_second, weights = panel_weights(
        a, if_ref[...], is_ref[...], up_ref[...], lt_ref[...], None, None
    )
    for k, (lo, hi) in enumerate(spans):
        top = min(hi, width)
        for c in range(lo, top, 512):
            w = min(512, top - c)
            value = q_refs[k][:, c - lo : c - lo + w].astype(f32) - dot(weights, p_ref[:, c : c + w])
            fresh[:, c : c + w] = (floor_residue(value) * scale).astype(bf16)

    @pl.when(info[1] == 0)
    def _():
        fresh[:, :256] = (lifted(l_first) * scale).astype(bf16)
        fresh[:, 256:512] = (lifted(l_second) * scale).astype(bf16)

    @pl.loop(0, count)
    def _(u):
        fetch(u).wait()

    slots = held.shape[0]
    for c in range(0, width, 256):
        spread = dot(spread_ref[...], fresh[:, c : c + 256]).astype(bf16)
        old = held[:, :, c : c + 256].reshape(slots * 8, 256)
        new = jnp.where(mask_ref[...] > 0, spread, old)
        held[:, :, c : c + 256] = new.reshape(slots, 8, 256)

    @pl.loop(0, count)
    def _(u):
        write(u).start()

    @pl.loop(0, count)
    def _(u):
        write(u).wait()


def merge(info, groups, spread, mask, pivots, small, parts, spans, out):
    slots = groups.shape[0]
    width = out.shape[1]
    vmem = pl.BlockSpec(memory_space=pltpu.VMEM)
    anywhere = pl.BlockSpec(memory_space=pl.ANY)
    operands = [spread, mask, pivots, *small, *parts, out]
    return pl.pallas_call(
        functools.partial(merge_kernel, spans),
        out_shape=jax.ShapeDtypeStruct(out.shape, bf16),
        grid_spec=pltpu.PrefetchScalarGridSpec(
            num_scalar_prefetch=2,
            grid=(1,),
            in_specs=[vmem] * (len(operands) - 1) + [anywhere],
            out_specs=anywhere,
            scratch_shapes=[
                pltpu.VMEM((slots, 8, width), bf16),
                pltpu.VMEM((slots, width), bf16),
                pltpu.SemaphoreType.DMA((slots,)),
                pltpu.SemaphoreType.DMA((slots,)),
            ],
        ),
        input_output_aliases={len(operands) + 1: 0},
        compiler_params=pltpu.CompilerParams(vmem_limit_bytes=56 << 20),
        cost_estimate=cheap,
        name="merge",
    )(info, groups, *operands)


def local(matrix, swaps, inverse_first, inverse_second):
    height, width = matrix.shape
    panel = inverse_first.shape[0]
    pivots = swaps.shape[0]
    col_count, depth_count, row_count = (
        lax.axis_size("col"), lax.axis_size("depth"), lax.axis_size("row"))
    count = col_count * depth_count
    levels = count.bit_length() - 1
    me = lax.axis_index("col") * depth_count + lax.axis_index("depth")
    row = lax.axis_index("row")
    first_row = me * height
    mean = pivots // count
    slots = -(-(mean + 4 * int(mean**0.5)) // 32) * 32

    def hop(value, bit):
        return lax.ppermute(value, blocks_axes, [(i, i ^ (1 << bit)) for i in range(count)])

    reaches = []
    while row_count >> (len(reaches) + 1):
        reaches.append(row_count >> (len(reaches) + 1))

    def row_hop(value, reach):
        pairs = [(i, i + reach) for i in range(0, row_count, 2 * reach)]
        got = lax.ppermute(value, "row", pairs)
        return jnp.where(row % (2 * reach) == reach, got, value)

    def along_row(value):
        for reach in reaches:
            value = row_hop(value, reach)
        return value

    together = lax.optimization_barrier

    orders = [[(k + s) % levels for k in range(levels)] for s in range(0, levels, -(-levels // 3))]
    spans = split_columns(width, [0.45, 0.18, 0.37])
    wide_spans = split_columns(width + pivots, [0.32, 0.34, 0.34])
    counts = [slots] + [slots << k for k in range(levels)]

    owner = swaps // height
    index = jnp.arange(pivots, dtype=jnp.int32)
    earlier = (owner[:, None] == owner[None, :]) & (index[None, :] < index[:, None])
    rank = jnp.sum(earlier.astype(jnp.int32), axis=1)
    rounds = jnp.max(rank) // slots + 1
    slot_index = jnp.arange(slots, dtype=jnp.int32)
    all_slots = jnp.arange(count * slots, dtype=jnp.int32)

    def round_slots(turn):
        place_in = rank - turn * slots
        valid = (place_in >= 0) & (place_in < slots)
        mine = (valid & (owner == me))[None, :] & (place_in[None, :] == slot_index[:, None])
        rows = jnp.sum(jnp.where(mine, (swaps - first_row)[None, :], 0), axis=1)
        used = jnp.any(mine, axis=1)
        return place_in, valid, rows, used

    def pivot_start(turn):
        place_in, valid, rows, used = round_slots(turn)
        lane = jnp.where(used, rows % 8, -1)[:, None]
        picked = pick(rows, lane, matrix, spans)
        relative = owner ^ me

        def key_of(order):
            ordered = sum(((relative >> bit) & 1) << k for k, bit in enumerate(order))
            return jnp.where(valid, ordered * slots + place_in, -1)

        keys = jnp.stack([key_of(order) for order in orders], axis=1)
        head_onehot = (key_of(range(levels))[:, None] == all_slots[None, :]).astype(bf16)
        return [[part] for part in picked], keys, head_onehot

    def join(pieces):
        return [held[0] if len(held) == 1 else jnp.concatenate(held, axis=0) for held in pieces]

    def pivot_hop(pieces, joined, level):
        return [
            held + [hop(part, order[level])] for held, part, order in zip(pieces, joined, orders)
        ]

    def head_hops(part):
        head = along_row(part)
        for level in range(levels):
            head = jnp.concatenate([head, hop(head, level)], axis=0)
        return head

    def flat(nested):
        return [value for held in nested for value in held]

    def swap_slabs(turn, top_panel):
        place_in, valid, _, _ = round_slots(turn)
        keys = []
        for order in orders:
            ordered = sum(((owner >> bit) & 1) << (levels - 1 - k) for k, bit in enumerate(order))
            keys.append(jnp.where(valid, ordered * slots + place_in, -1))
        at = jnp.stack([first_row])
        return [
            source(at, key[None, :], top_panel, matrix, span, counts)
            for key, span in zip(keys, wide_spans)
        ]

    def swap_hop(slabs, level):
        result = []
        for order, (own, *leaving) in zip(orders, slabs):
            bit = order[level]
            reached = [0]
            for done in order[:level]:
                reached += [i | (1 << done) for i in reached]
            got = lax.ppermute(leaving[-1], blocks_axes, [(i, i | (1 << bit)) for i in reached])
            took = (me >> bit) & 1 == 1
            kept = [
                jnp.where(took, got[(slots << k) : (slots << (k + 1))], leaving[k])
                for k in range(levels - 1 - level)
            ]
            result.append([jnp.where(took, got[:slots], own), *kept])
        return result

    def swap_tables(turn):
        _, _, rows, used = round_slots(turn)
        group = jnp.where(used, rows // 8, -1 - slot_index)
        same = group[:, None] == group[None, :]
        before = slot_index[None, :] < slot_index[:, None]
        lead = used & ~jnp.any(same & before, axis=1)
        lead_rank = jnp.sum((lead[None, :] & before).astype(jnp.int32), axis=1)
        at = jnp.sum(jnp.where(same & lead[None, :], lead_rank[None, :], 0), axis=1)
        chosen = lead[None, :] & (lead_rank[None, :] == slot_index[:, None])
        groups = jnp.sum(jnp.where(chosen, group[None, :], 0), axis=1)
        position = jnp.where(used, at * 8 + rows % 8, -1)
        spread = (jnp.arange(slots * 8)[:, None] == position[None, :]).astype(bf16)
        mask = jnp.max(spread, axis=1, keepdims=True)
        return groups, jnp.sum(lead.astype(jnp.int32)), spread, mask

    tile = 256 if height % 1280 == 0 else 128
    def panel_hops(lo, hi, *after):
        value = matrix[lo:hi, :pivots]
        far = row_hop(tie(value, *after) if after else value, reaches[0])
        near = far
        for reach in reaches[1:]:
            near = row_hop(near, reach)
        return far, near

    def near_of(value):
        for reach in reaches[1:]:
            value = row_hop(value, reach)
        return value

    middle = pivots + (height - pivots) // 2
    first_far = row_hop(matrix[:pivots, :pivots], reaches[0])
    pieces, keys, head_onehot = pivot_start(0)
    head_part = pieces[0][0][:, :pivots]
    for level in range(levels - 1):
        joined = join(pieces)
        if level == 1:
            joined, first_far = together((joined, first_far))
        pieces = pivot_hop(pieces, joined, level)
    second, first_far = together((matrix[pivots:middle, :pivots], first_far))
    second_far = row_hop(second, reaches[0])
    third, second_far = together((matrix[middle:, :pivots], second_far))
    third_far = row_hop(third, reaches[0])
    joined, second_far = together((join(pieces), second_far))
    first_near = near_of(first_far)
    slabs = swap_slabs(0, first_near)
    pieces = pivot_hop(pieces, joined, levels - 1)
    pieces, third_far, slabs = together((pieces, third_far, slabs))
    second_near = near_of(second_far)
    third_near = near_of(third_far)
    slabs = swap_hop(slabs, 0)
    pivot_rows = place(keys, flat(pieces), spans)
    pivot_head = dot(head_onehot, head_hops(head_part)).astype(bf16)

    def more_pivots(state):
        turn, rows_, head_ = state
        pieces, keys, head_onehot = pivot_start(turn)
        for level in range(levels):
            pieces = pivot_hop(pieces, join(pieces), level)
        extra_head = dot(head_onehot, head_hops(pieces[0][0][:, :pivots])).astype(bf16)
        return turn + 1, rows_ + place(keys, flat(pieces), spans), head_ + extra_head

    _, pivot_rows, pivot_head = lax.while_loop(
        lambda s: s[0] < rounds, more_pivots, (jnp.int32(1), pivot_rows, pivot_head))

    upper = pivot_head[:panel, panel:]
    l_top = centred(dot(pivot_head[panel:, :panel], inverse_first)).astype(bf16)
    small = [inverse_first, inverse_second, upper, l_top]
    info = jnp.stack([first_row, row]).astype(jnp.int32)
    panel_all = jnp.concatenate([first_near, second_near, third_near], axis=0)
    weights, head = weights_of(info, 0, tile, panel_all, [pivot_head, *small])
    cuts = [height * k // 5 // tile * tile for k in (0, 2, 4, 5)]
    mark = jnp.zeros((8, 128), f32)
    out = None
    for k, (lo, hi) in enumerate(zip(cuts[:-1], cuts[1:])):
        out, mark = update(info, mark, lo, hi - lo, tile, weights, head, matrix, pivot_rows, out)
        if k + 1 < min(levels, 3):
            slabs, mark = together((slabs, mark))
            slabs = swap_hop(slabs, k + 1)
    for level in range(3, levels):
        slabs = swap_hop(slabs, level)

    def merged(turn, out, slabs, mark):
        parts = [own[0] for own in slabs]
        groups, used, spread, mask = swap_tables(turn)
        info = jnp.stack([first_row, row, used + mark[0, 0].astype(jnp.int32)]).astype(jnp.int32)
        return merge(info, groups, spread, mask, pivot_rows, small, parts, wide_spans, out)

    out = merged(0, out, slabs, mark)

    def more_swapped(state):
        turn, out = state
        slabs = swap_slabs(turn, first_near)
        for level in range(levels):
            slabs = swap_hop(slabs, level)
        return turn + 1, merged(turn, out, slabs, mark)

    _, out = lax.while_loop(lambda s: s[0] < rounds, more_swapped, (jnp.int32(1), out))
    return out


def solution(mesh):
    return jax.shard_map(
        local,
        mesh=mesh,
        in_specs=(P(("col", "depth"), "row"), P(), P(), P()),
        out_specs=P(("col", "depth"), "row"),
        check_vma=False,
    )
```
